512 devices in a mesh: flop: 4 (over x), turn: 16 (over y, core), river: 8 (over z).
Axes of the slice: x: 4, y: 8, z: 8, core: 2. Of those that a mesh axis runs over, the one named last changes fastest.
Arguments:
- regrets: float32 [4, 256, 1326], P('flop', ('turn', 'river')), may hold values from -6 to 6
- opp_reach: bfloat16 [4, 256, 1326], P('flop', ('turn', 'river')), may hold values from 0 to 1
- pot_size: int32 [4, 256], P('flop', ('turn', 'river')), may hold values from 1 to 8
- line_kind: int32 [4, 256], P('flop', ('turn', 'river')), may hold values from 0 to 2
- board_lines: int32 [4, 16, 16, 256], P('flop', 'turn', 'river'), may hold values from 0 to 255, as said below
- board_count: int32 [4, 16, 16], P('flop', 'turn', 'river'), may hold values from 64 to 256, as said below
- hand_ranks: int32 [4, 16, 16, 1326], P('flop', 'turn', 'river'), may hold values from 0 to 7461
- live_hands: int32 [4, 16, 16, 1326], P('flop', 'turn', 'river'), may hold values 0 or 1
Outputs:
- new_regrets: float32 [4, 256, 1326], P('flop', ('turn', 'river'))
- chance_values: float32 [128, 1326], P(('turn', 'river'))
The draws below stay inside these ranges and needn't reach their ends.
Inputs may be any that keep to these rules, and one draw needn't show every extreme that they name: `board_lines`: each board lists 256 different lines of its flop; its first board_count slots hold the lines live on it, the other slots add nothing. `board_count`: in every flop one board has all 256 slots live and another only 64.
All inputs are finite; a program needn't handle non-finite values. No bound on the sum of `live_hands` on one device may be relied on, other than what follows from the above.
Results may differ from the reference program's by a relative error of at most 0.0003.
Values may be sent and summed in bfloat16 or wider, within the bound.
A program may use at most 64 MiB of HBM per device.

```python
import jax
import jax.numpy as jnp
import numpy as np
from jax import lax

CARDS = 52
H = 1326
ACTS = 2
LINES = 256
CAP = 256
FLOPS = 4
TURNS = 16
RIVERS = 16
N_FLOP = 4


def draw_board_lines(key, part):
    board_total = FLOPS * TURNS * RIVERS
    line_keys = jax.random.split(jax.random.fold_in(key, 11), board_total)
    orders = jax.vmap(lambda board_key: jax.random.permutation(board_key, LINES)[:CAP])(line_keys)
    return orders.reshape(FLOPS, TURNS, RIVERS, CAP).astype(jnp.int32)


def draw_board_count(key, part):
    board_total = TURNS * RIVERS
    live_counts = jax.random.randint(jax.random.fold_in(key, 23), (FLOPS, board_total), CAP // 4, CAP + 1)
    full_board = jax.random.randint(jax.random.fold_in(key, 29), (FLOPS, 1), 0, board_total)
    light_step = jax.random.randint(jax.random.fold_in(key, 31), (FLOPS, 1), 1, max(board_total, 2))
    light_board = (full_board + light_step) % board_total
    board_index = jnp.arange(board_total, dtype=jnp.int32)[None, :]
    live_counts = jnp.where(board_index == light_board, CAP // 4, live_counts)
    live_counts = jnp.where(board_index == full_board, CAP, live_counts)
    return live_counts.reshape(FLOPS, TURNS, RIVERS).astype(jnp.int32)


def place_ends(entries, rng, low, top_value):
    longest = entries.shape.index(max(entries.shape))
    spots = []
    for shift in (0, 1):
        where = [jax.random.randint(jax.random.fold_in(rng, axis), (), 0, length) for axis, length in enumerate(entries.shape)]
        where[longest] = (where[longest] + shift) % entries.shape[longest]
        spots.append(tuple(where))
    return entries.at[spots[0]].set(low).at[spots[1]].set(top_value)


def block_scale(own_key, dims, pieces, least, top_value):
    gain, own = 1.0, jax.random.fold_in(own_key, 6)
    for position, blocks in pieces:
        heights = jnp.exp(jax.random.uniform(jax.random.fold_in(own, position), (blocks,), jnp.float32, least / len(pieces), top_value / len(pieces)))
        gain = gain * jnp.repeat(heights, dims[position] // blocks).reshape([-1 if axis == position else 1 for axis in range(len(dims))])
    return gain


def gaussian(stream_key, shape, width, limit, pieces=(), held_as=jnp.bfloat16):
    level = block_scale(stream_key, shape, pieces, -0.22, 0.18) if pieces else 1.0
    array = jax.random.normal(stream_key, shape, jnp.float32) * width * level
    return jnp.minimum(jnp.maximum(array, -limit), limit).astype(held_as)


def setup_inputs(seed: int = 0) -> dict:
    keys = jax.random.split(jax.random.key(seed), 9)
    return {
        "regrets": gaussian(keys[0], (FLOPS, LINES, H), 1.0, 6.0, ((0, 4), (1, 128)), jnp.float32),
        "opp_reach": jnp.clip(1.0 * jax.random.uniform(keys[1], (FLOPS, LINES, H), jnp.float32) ** block_scale(keys[1], (FLOPS, LINES, H), ((0, 4), (1, 128)), -0.2, 0.2), 0.0, 1.0).astype(jnp.bfloat16),
        "pot_size": place_ends(jax.random.randint(keys[2], (FLOPS, LINES), 1, 9), jax.random.fold_in(keys[2], 1), 1, 8).astype(jnp.int32),
        "line_kind": place_ends(jax.random.randint(keys[3], (FLOPS, LINES), 0, 3), jax.random.fold_in(keys[3], 1), 0, 2).astype(jnp.int32),
        "board_lines": draw_board_lines(jax.random.fold_in(keys[8], 71), 0),
        "board_count": draw_board_count(jax.random.fold_in(keys[8], 71), 0),
        "hand_ranks": place_ends(jax.random.randint(keys[6], (FLOPS, TURNS, RIVERS, H), 0, 7462), jax.random.fold_in(keys[6], 1), 0, 7461).astype(jnp.int32),
        "live_hands": place_ends((jax.random.randint(keys[7], (FLOPS, TURNS, RIVERS, H), 0, 1000) < 815).astype(jnp.int32), jax.random.fold_in(keys[7], 1), 0, 1),
    }


floor_share = 0.1


def disjoint_table(card_count):
    card_first, card_second = np.triu_indices(card_count, 1)
    first_cards = jnp.asarray(card_first.astype(np.int32))
    second_cards = jnp.asarray(card_second.astype(np.int32))
    apart = (first_cards[:, None] != first_cards[None, :]) & (first_cards[:, None] != second_cards[None, :])
    apart = apart & (second_cards[:, None] != first_cards[None, :]) & (second_cards[:, None] != second_cards[None, :])
    return apart


def payoff_matrix(board_ranks, board_live, apart):
    both_live = apart & (board_live[:, None] > 0) & (board_live[None, :] > 0)
    fold_part = both_live.astype(jnp.float32)
    ordering = jnp.sign(board_ranks[None, :] - board_ranks[:, None]).astype(jnp.float32)
    return jnp.concatenate([fold_part * ordering, fold_part], axis=1)


def reference(regrets, opp_reach, pot_size, line_kind, board_lines, board_count, hand_ranks, live_hands):
    hand_count = opp_reach.shape[2]
    apart = disjoint_table(CARDS)
    chance_scale = 1.0 / (TURNS * RIVERS * hand_count)
    pot_float = pot_size.astype(jnp.float32)
    show_coef = jnp.where(line_kind == 0, pot_float, 0.0)
    fold_coef = jnp.where(line_kind == 1, -pot_float, jnp.where(line_kind == 2, pot_float, 0.0))
    slot_index = jnp.arange(CAP, dtype=jnp.int32)
    flop_values = []
    for flop_index in range(N_FLOP):
        reach_rows = opp_reach[flop_index].astype(jnp.float32)
        line_coef = jnp.stack([show_coef[flop_index], fold_coef[flop_index]], axis=1)

        def add_board(running, board_item):
            slot_lines, live_count, board_ranks, board_live = board_item
            matrix = payoff_matrix(board_ranks, board_live, apart)
            slot_reach = jnp.take(reach_rows, slot_lines, axis=0)
            products = jnp.dot(slot_reach, matrix, precision=lax.Precision.HIGHEST)
            slot_coef = jnp.take(line_coef, slot_lines, axis=0)
            keep_mask = (slot_index < live_count).astype(jnp.float32)
            board_value = (slot_coef[:, 0:1] * products[:, :hand_count] + slot_coef[:, 1:2] * products[:, hand_count:]) * (chance_scale * keep_mask)[:, None]
            return running.at[slot_lines].add(board_value), None

        items = (board_lines[flop_index].reshape(-1, CAP), board_count[flop_index].reshape(-1),
                 hand_ranks[flop_index].reshape(-1, hand_count), live_hands[flop_index].reshape(-1, hand_count))
        summed, _ = lax.scan(add_board, jnp.zeros((LINES, hand_count), jnp.float32), items)
        flop_values.append(summed)
    line_values = jnp.stack(flop_values)
    grouped = regrets.reshape(N_FLOP, LINES // ACTS, ACTS, hand_count)
    worth_lines = line_values.reshape(N_FLOP, LINES // ACTS, ACTS, hand_count)
    positive = jnp.maximum(grouped, 0.0)
    strategy = (positive + floor_share) / (jnp.sum(positive, axis=2, keepdims=True) + ACTS * floor_share)
    node_values = jnp.sum(strategy * worth_lines, axis=2)
    new_regrets = jnp.maximum(grouped + worth_lines - node_values[:, :, None, :], 0.0).reshape(regrets.shape)
    chance_values = jnp.sum(node_values, axis=0) / N_FLOP
    return (new_regrets, chance_values)
```

```python
import functools

import jax
import jax.numpy as jnp
import numpy as np
from jax import lax
from jax.experimental import pallas as pl
from jax.experimental.pallas import tpu as pltpu
from jax.sharding import PartitionSpec as P

CARDS = 52
H = 1326
LANES = 128
HP = 1408
TILES = HP // LANES
SPLIT = 768
BOARDS = 256
FLOOR = 0.1
N = 8
MESH = pl.DeviceIdType.MESH
BF16 = jnp.bfloat16
F32 = jnp.float32

CHUNKS = ((0, 0, 256), (1, 768, 256), (0, 256, 256), (1, 1024, 256), (0, 512, 256), (1, 1280, 128))


def card_tables():
    first, second = np.triu_indices(CARDS, 1)
    hands = np.arange(H)
    left = np.zeros((HP, LANES), np.float32)
    left[hands, first] = -1.0
    left[hands, second] = -1.0
    left[:, CARDS] = 1.0
    right = np.zeros((LANES, HP), np.float32)
    right[first, hands] = 1.0
    right[second, hands] = 1.0
    right[CARDS, :] = 1.0
    return left.astype(BF16), right.astype(BF16)


def kernel(
    regrets, reach, pot, kind, lines, count, ranks, live, cards_left, cards_right,
    new_regrets, chance,
    apart, show, held, board, col_hi, col_lo, row_hi, row_lo, row_lv, keep, lhs_show, lhs_fold,
    part, recv1, mid, recv2, node,
    sem_board, ag_send, ag_recv, rs1_send, rs1_recv, rs2_send, rs2_recv, fl_send, fl_recv,
):
    f = lax.axis_index("flop")
    t = lax.axis_index("turn")
    z = lax.axis_index("river")
    y = t // 2
    c = t % 2

    def z_peer(d):
        return lax.rem(z + d, N)

    def y_peer(d):
        return lax.rem(y + d, N)

    def on_z(d):
        return (f, t, z_peer(d))

    def on_y(d):
        return (f, 2 * y_peer(d) + c, z)

    other_core = (f, 2 * y + (1 - c), z)

    barrier = pltpu.get_barrier_semaphore()
    for d in range(1, N):
        pl.semaphore_signal(barrier, inc=1, device_id=on_z(d), device_id_type=MESH)
        pl.semaphore_signal(barrier, inc=1, device_id=on_y(d), device_id_type=MESH)
    pl.semaphore_signal(barrier, inc=1, device_id=other_core, device_id_type=MESH)
    for d in range(1, 4):
        pl.semaphore_signal(barrier, inc=1, device_id=(lax.rem(f + d, 4), t, z), device_id_type=MESH)

    held[y, z] = jnp.zeros((2, HP), BF16)
    held[y, z, :, 0:H] = reach[...]
    row_id = lax.broadcasted_iota(jnp.int32, (2, LANES), 0)
    lane_id = lax.broadcasted_iota(jnp.int32, (2, LANES), 1)
    flag0 = jnp.where(kind[0, 0] == 0, 1.0, 0.0).astype(F32)
    flag1 = jnp.where(kind[0, 1] == 0, 1.0, 0.0).astype(F32)
    flags = jnp.where(lane_id == H - (TILES - 1) * LANES, jnp.where(row_id == 0, flag0, flag1), 0.0)
    tail = held[y, z, :, (TILES - 1) * LANES : HP].astype(F32)
    held[y, z, :, (TILES - 1) * LANES : HP] = (tail + flags).astype(BF16)

    board[0] = jnp.zeros((8, HP), F32)
    rank_high = (ranks[...] >> 7) << 7
    board[0, 0:2, 0:H] = rank_high.astype(F32)
    board[0, 2:4, 0:H] = (ranks[...] - rank_high).astype(F32)
    board[0, 4:6, 0:H] = live[...].astype(F32)
    slot_row = lax.broadcasted_iota(jnp.int32, (2, 256), 0)
    slot_id = lax.broadcasted_iota(jnp.int32, (2, 256), 1)
    limit = jnp.where(slot_row == 0, count[0], count[1])
    board[0, 6:8, 0:256] = jnp.where(slot_id < limit, lines[...], -1).astype(F32)

    pl.semaphore_wait(barrier, 18)

    def remote(src, dst, send, recv, device):
        copy = pltpu.make_async_remote_copy(
            src_ref=src, dst_ref=dst, send_sem=send, recv_sem=recv, device_id=device, device_id_type=MESH
        )
        copy.start()
        return copy

    board_copy = remote(board.at[0], board.at[1], sem_board.at[0], sem_board.at[1], other_core)
    ag1 = []
    for d in range(1, N):
        own = held.at[y, z, :, 0:SPLIT]
        ag1.append(remote(own, own, ag_send.at[0, d], ag_recv.at[0, d], on_z(d)))
        own = held.at[y, z, :, SPLIT:HP]
        ag1.append(remote(own, own, ag_send.at[1, d], ag_recv.at[1, d], on_y(d)))

    def spread(i, carry):
        rows = pl.ds(pl.multiple_of(i * 128, 128), 128)
        for first, width in ((0, 512), (512, 512), (1024, 384)):
            cols = slice(first, first + width)
            free = jnp.dot(cards_left[rows, :], cards_right[:, cols], preferred_element_type=F32)
            apart[rows, cols] = jnp.maximum(free, 0.0).astype(BF16)
        return carry

    lax.fori_loop(0, TILES, spread, 0)

    def prepare(s):
        for k in range(2):
            b = 2 * s + k
            for j in range(TILES):
                cols = slice(j * LANES, (j + 1) * LANES)
                col_hi[b, cols, :] = jnp.broadcast_to(board[s, k : k + 1, cols], (LANES, LANES)).T.astype(BF16)
                col_lo[b, cols, :] = jnp.broadcast_to(board[s, 2 + k : 3 + k, cols], (LANES, LANES)).T.astype(BF16)
            row_hi[b] = jnp.broadcast_to(board[s, k : k + 1, :], (16, HP)).astype(BF16)
            row_lo[b] = jnp.broadcast_to(board[s, 2 + k : 3 + k, :], (16, HP)).astype(BF16)
            row_lv[b] = jnp.broadcast_to(board[s, 4 + k : 5 + k, :], (16, HP)).astype(BF16)
            row = lax.broadcasted_iota(jnp.int32, (128, 256), 0)
            line_a = 32 * ((row // 2) % 8) + 16 * c + 2 * (row // 16) + row % 2
            line_b = 32 * (row // 16) + 16 * c + row % 16
            slots = jnp.broadcast_to(board[s, 6 + k : 7 + k, 0:256], (128, 256))
            for o, line in enumerate((line_a, line_b)):
                hit = jnp.where(slots == line.astype(F32), 1.0, 0.0)
                keep[o, b] = jnp.broadcast_to(jnp.sum(hit, axis=1, keepdims=True), (128, LANES)).astype(BF16)

    def generate(s):
        def step(i, carry):
            rows = pl.ds(pl.multiple_of(i * 16, 16), 16)
            for k in range(2):
                b = 2 * s + k
                hi = col_hi[b, rows, :]
                lo = col_lo[b, rows, :]
                for j in range(TILES):
                    cols = slice(j * LANES, (j + 1) * LANES)
                    bound = row_lv[b, :, cols]
                    gap = ((row_hi[b, :, cols] - hi) + (row_lo[b, :, cols] - lo)) * apart[rows, cols]
                    show[b, rows, cols] = jnp.maximum(jnp.minimum(gap, bound), -bound)
            return carry

        lax.fori_loop(0, HP // 16, step, 0)

    prepare(0)
    generate(0)

    for copy in ag1:
        copy.wait_recv()
    ag2 = []
    for d in range(1, N):
        row = held.at[y, :, :, 0:SPLIT]
        ag2.append(remote(row, row, ag_send.at[2, d], ag_recv.at[2, d], on_y(d)))
        column = held.at[:, z, :, SPLIT:HP]
        ag2.append(remote(column, column, ag_send.at[3, d], ag_recv.at[3, d], on_z(d)))

    board_copy.wait_recv()
    prepare(1)
    generate(1)

    for copy in ag2:
        copy.wait_recv()

    tail_lane = lax.broadcasted_iota(jnp.int32, (16, LANES), 1)

    def build(i, carry):
        for o in range(2):
            block = held[:, i] if o == 0 else held[i]
            block = block.reshape(16, HP)
            rows = pl.ds(pl.multiple_of(i * 16, 16), 16)
            tail = block[:, (TILES - 1) * LANES : HP].astype(F32)
            tail = jnp.where(tail_lane == H - (TILES - 1) * LANES, tail, 0.0)
            flag = jnp.broadcast_to(jnp.sum(tail, axis=1, keepdims=True), (16, LANES)).astype(BF16)
            for b in range(4):
                kept = keep[o, b, rows, :]
                fold_rows = pl.ds(pl.multiple_of(b * 128 + i * 16, 16), 16)
                for j in range(TILES):
                    cols = slice(j * LANES, (j + 1) * LANES)
                    masked = block[:, cols] * kept * row_lv[b, :, cols]
                    shown = masked * flag
                    lhs_show[o, b, rows, cols] = shown
                    lhs_fold[o, fold_rows, cols] = masked - shown
        return carry

    lax.fori_loop(0, N, build, 0)

    rs1 = []
    for n, (o, first, width) in enumerate(CHUNKS):
        cols = slice(first, first + width)
        folded = jnp.dot(lhs_fold[o], apart[:, cols], preferred_element_type=F32)
        total = jnp.dot(lhs_show[o, 0], show[0, :, cols], preferred_element_type=F32)
        for b in range(1, 4):
            total += jnp.dot(lhs_show[o, b], show[b, :, cols], preferred_element_type=F32)
        for b in range(4):
            total += folded[b * 128 : (b + 1) * 128] * board[b // 2, 4 + b % 2 : 5 + b % 2, cols]
        part[n, :, 0:width] = total
        copies = []
        for d in range(1, N):
            target = z_peer(d) if o == 0 else y_peer(d)
            src = part.at[n, pl.ds(pl.multiple_of(target * 16, 16), 16), 0:width]
            copies.append(
                remote(src, recv1.at[n, d, :, 0:width], rs1_send.at[n, d], rs1_recv.at[n, d], on_z(d) if o == 0 else on_y(d))
            )
        rs1.append(copies)

    rs2 = []
    for n, (o, first, width) in enumerate(CHUNKS):
        mine = z if o == 0 else y
        total = part[n, pl.ds(pl.multiple_of(mine * 16, 16), 16), 0:width]
        for d in range(1, N):
            rs1[n][d - 1].wait_recv()
        for d in range(1, N):
            total += recv1[n, d, :, 0:width]
        for q in range(N):
            mid[q, :, first : first + width] = total[2 * q : 2 * q + 2]
        if n >= len(CHUNKS) - 2:
            cols = slice(0, SPLIT) if o == 0 else slice(SPLIT, HP)
            for d in range(1, N):
                target = y_peer(d) if o == 0 else z_peer(d)
                rs2.append(
                    remote(
                        mid.at[target, :, cols], recv2.at[d, :, cols], rs2_send.at[o, d], rs2_recv.at[o, d],
                        on_y(d) if o == 0 else on_z(d),
                    )
                )
    for copy in rs2:
        copy.wait_recv()
    value_a = mid[y, :, 0:SPLIT]
    value_b = mid[z, :, SPLIT:H]
    for d in range(1, N):
        value_a += recv2[d, :, 0:SPLIT]
        value_b += recv2[d, :, SPLIT:H]
    row_id = lax.broadcasted_iota(jnp.int32, (2, LANES), 0)
    pots = [pot[0, a].astype(F32) for a in range(2)]
    coefs = [jnp.where(kind[0, a] == 1, -pots[a], pots[a]) * (1.0 / (BOARDS * H)) for a in range(2)]
    coef = jnp.where(row_id == 0, coefs[0], coefs[1])[:, 0:1]
    for first, last, value in ((0, SPLIT, value_a), (SPLIT, H, value_b)):
        worth = value * coef
        held_regret = regrets[:, first:last]
        positive = jnp.maximum(held_regret, 0.0)
        strategy = (positive + FLOOR) / (jnp.sum(positive, axis=0, keepdims=True) + 2 * FLOOR)
        decision = jnp.sum(strategy * worth, axis=0, keepdims=True)
        new_regrets[:, first:last] = jnp.maximum(held_regret + worth - decision, 0.0)
        node[f, :, first:last] = decision

    flops = []
    for d in range(1, 4):
        own = node.at[f]
        flops.append(remote(own, own, fl_send.at[d], fl_recv.at[d], (lax.rem(f + d, 4), t, z)))
    for copy in flops:
        copy.wait_recv()
    chance[...] = ((node[0] + node[1]) + (node[2] + node[3])) * 0.25

    board_copy.wait_send()
    for copy in ag1 + ag2 + rs2 + flops:
        copy.wait_send()
    for copies in rs1:
        for copy in copies:
            copy.wait_send()


def on_device(regrets, opp_reach, pot_size, line_kind, board_lines, board_count, hand_ranks, live_hands):
    vmem = pl.BlockSpec(memory_space=pltpu.VMEM)
    smem = pl.BlockSpec(memory_space=pltpu.SMEM)
    dma = pltpu.SemaphoreType.DMA
    left, right = card_tables()
    updated, chance = pl.pallas_call(
        kernel,
        out_shape=(jax.ShapeDtypeStruct((2, H), F32), jax.ShapeDtypeStruct((1, H), F32)),
        in_specs=[vmem, vmem, smem, smem, vmem, smem, vmem, vmem, vmem, vmem],
        out_specs=(vmem, vmem),
        scratch_shapes=[
            pltpu.VMEM((HP, HP), BF16),
            pltpu.VMEM((4, HP, HP), BF16),
            pltpu.VMEM((N, N, 2, HP), BF16),
            pltpu.VMEM((2, 8, HP), F32),
            pltpu.VMEM((4, HP, LANES), BF16),
            pltpu.VMEM((4, HP, LANES), BF16),
            pltpu.VMEM((4, 16, HP), BF16),
            pltpu.VMEM((4, 16, HP), BF16),
            pltpu.VMEM((4, 16, HP), BF16),
            pltpu.VMEM((2, 4, 128, LANES), BF16),
            pltpu.VMEM((2, 4, 128, HP), BF16),
            pltpu.VMEM((2, 512, HP), BF16),
            pltpu.VMEM((6, 128, 256), F32),
            pltpu.VMEM((6, N, 16, 256), F32),
            pltpu.VMEM((N, 2, HP), F32),
            pltpu.VMEM((N, 2, HP), F32),
            pltpu.VMEM((4, 1, H), F32),
            dma((2,)),
            dma((4, N)),
            dma((4, N)),
            dma((6, N)),
            dma((6, N)),
            dma((2, N)),
            dma((2, N)),
            dma((4,)),
            dma((4,)),
        ],
        compiler_params=pltpu.CompilerParams(
            collective_id=0, has_side_effects=True, vmem_limit_bytes=48 * 1024 * 1024
        ),
    )(
        regrets[0], opp_reach[0], pot_size, line_kind, board_lines[0, 0], board_count[0, 0],
        hand_ranks[0, 0], live_hands[0, 0], jnp.asarray(left), jnp.asarray(right),
    )
    return updated[None], chance


def solution(mesh):
    lines = ("turn", "river")
    placed = (
        P("flop", lines, None),
        P("flop", lines, None),
        P("flop", lines),
        P("flop", lines),
        P("flop", "turn", "river", None),
        P("flop", "turn", "river"),
        P("flop", "turn", "river", None),
        P("flop", "turn", "river", None),
    )
    return jax.shard_map(
        on_device,
        mesh=mesh,
        in_specs=placed,
        out_specs=(P("flop", lines, None), P(lines, None)),
        check_vma=False,
    )
```

```python
import functools

import jax
import jax.numpy as jnp
import numpy as np
from jax import lax
from jax.experimental import pallas as pl
from jax.experimental.pallas import tpu as pltpu
from jax.sharding import PartitionSpec as P

CARDS = 52
H = 1326
LANES = 128
HP = 1408
TILES = HP // LANES
SPLIT = 768
TAIL = HP - LANES
FLAG_LANE = H - TAIL
BOARDS = 256
FLOOR = 0.1
N = 8
PARTS = (0, 128, 192)
MESH = pl.DeviceIdType.MESH
BF16 = jnp.bfloat16
F32 = jnp.float32

CHUNKS = ((0, 0, 256), (1, 768, 256), (0, 256, 256), (1, 1024, 256), (0, 512, 256), (1, 1280, 128))


def card_tables():
    first, second = np.triu_indices(CARDS, 1)
    hands = np.arange(H)
    left = np.zeros((HP, 256), np.float32)
    right = np.zeros((256, HP), np.float32)
    for start in PARTS:
        left[hands, start + first] = -1.0
        left[hands, start + second] = -1.0
        left[:, start + CARDS] = 1.0
        right[start + first, hands] = 1.0
        right[start + second, hands] = 1.0
        right[start + CARDS, :] = 1.0
    return left.astype(BF16), right.astype(BF16)


def kernel(*refs):
    sources, (new_regrets, chance), inputs, rest = refs[0:10], refs[10:12], refs[12:22], refs[22:]
    regrets, reach, pot, kind, lines, count, ranks, live, cards_left, cards_right = inputs
    (
        apart, minus_apart, show, line_a, line_b, rows_a, rows_b, board, col_hi, col_lo, row_hi, row_lo, row_lv,
        keep, raw, lhs_show, lhs_fold, sums,
        part, recv1, mid, recv2, node,
        sem_in, sem_board, ag_send, ag_recv, rs1_send, rs1_recv, rs2_send, rs2_recv, fl_send, fl_recv,
    ) = rest
    f = lax.axis_index("flop")
    t = lax.axis_index("turn")
    z = lax.axis_index("river")
    y = t // 2
    c = t % 2

    def z_peer(d):
        return lax.rem(z + d, N)

    def y_peer(d):
        return lax.rem(y + d, N)

    def on_z(d):
        return (f, t, z_peer(d))

    def on_y(d):
        return (f, 2 * y_peer(d) + c, z)

    other_core = (f, 2 * y + (1 - c), z)

    loads = [pltpu.make_async_copy(sources[k], inputs[k], sem_in.at[k]) for k in range(10)]
    for load in loads:
        load.start()

    barrier = pltpu.get_barrier_semaphore()
    for d in range(1, N):
        pl.semaphore_signal(barrier, inc=1, device_id=on_z(d), device_id_type=MESH)
        pl.semaphore_signal(barrier, inc=1, device_id=on_y(d), device_id_type=MESH)
    pl.semaphore_signal(barrier, inc=1, device_id=other_core, device_id_type=MESH)
    for d in range(1, 4):
        pl.semaphore_signal(barrier, inc=1, device_id=(lax.rem(f + d, 4), t, z), device_id_type=MESH)

    for load in loads:
        load.wait()

    row_id = lax.broadcasted_iota(jnp.int32, (2, LANES), 0)
    lane_id = lax.broadcasted_iota(jnp.int32, (2, LANES), 1)
    flag0 = jnp.where(kind[0, 0] == 0, 1.0, 0.0).astype(F32)
    flag1 = jnp.where(kind[0, 1] == 0, 1.0, 0.0).astype(F32)
    flags = jnp.where(lane_id == FLAG_LANE, jnp.where(row_id == 0, flag0, flag1), 0.0)
    line_a[z] = reach[:, 0:SPLIT]
    line_b[y] = jnp.zeros((2, HP - SPLIT), BF16)
    line_b[y, :, 0 : H - SPLIT] = reach[:, SPLIT:H]
    tail = line_b[y, :, TAIL - SPLIT : HP - SPLIT].astype(F32)
    line_b[y, :, TAIL - SPLIT : HP - SPLIT] = (tail + flags).astype(BF16)

    board[0] = jnp.zeros((8, HP), F32)
    rank_high = (ranks[...] >> 7) << 7
    board[0, 0:2, 0:H] = rank_high.astype(F32)
    board[0, 2:4, 0:H] = (ranks[...] - rank_high).astype(F32)
    board[0, 4:6, 0:H] = live[...].astype(F32)
    slot_row = lax.broadcasted_iota(jnp.int32, (2, 256), 0)
    slot_id = lax.broadcasted_iota(jnp.int32, (2, 256), 1)
    limit = jnp.where(slot_row == 0, count[0, 0], count[0, 1])
    board[0, 6:8, 0:256] = jnp.where(slot_id < limit, lines[...], -1).astype(F32)

    def spread(i, carry):
        rows = pl.ds(pl.multiple_of(i * 128, 128), 128)
        for first, width in ((0, 512), (512, 512), (1024, 384)):
            cols = slice(first, first + width)
            free = jnp.dot(cards_left[rows, 0:128], cards_right[0:128, cols], preferred_element_type=F32)
            free = jnp.maximum(free, 0.0).astype(BF16)
            apart[rows, cols] = free
            minus_apart[rows, cols] = -free
        return carry

    lax.fori_loop(0, TILES, spread, 0)

    def prepare(s):
        for k in range(2):
            b = 2 * s + k
            for j in range(TILES):
                cols = slice(j * LANES, (j + 1) * LANES)
                col_hi[b, cols, :] = jnp.broadcast_to(board[s, k : k + 1, cols], (LANES, LANES)).T.astype(BF16)
                col_lo[b, cols, :] = jnp.broadcast_to(board[s, 2 + k : 3 + k, cols], (LANES, LANES)).T.astype(BF16)
            row_hi[b] = jnp.broadcast_to(board[s, k : k + 1, :], (16, HP)).astype(BF16)
            row_lo[b] = jnp.broadcast_to(board[s, 2 + k : 3 + k, :], (16, HP)).astype(BF16)
            row_lv[b] = jnp.broadcast_to(board[s, 4 + k : 5 + k, :], (16, HP)).astype(BF16)
            row = lax.broadcasted_iota(jnp.int32, (128, 256), 0)
            in_a = 32 * ((row // 2) % 8) + 16 * c + 2 * (row // 16) + row % 2
            in_b = 32 * (row // 16) + 16 * c + row % 16
            slots = jnp.broadcast_to(board[s, 6 + k : 7 + k, 0:256], (128, 256))
            for o, line in enumerate((in_a, in_b)):
                hit = jnp.where(slots == line.astype(F32), 1.0, 0.0)
                keep[o, b] = jnp.broadcast_to(jnp.sum(hit, axis=1, keepdims=True), (128, LANES)).astype(BF16)

    def generate(s):
        def step(i, carry):
            rows = pl.ds(pl.multiple_of(i * 64, 64), 64)
            for j in range(TILES):
                cols = slice(j * LANES, (j + 1) * LANES)
                bound = apart[rows, cols]
                minus_bound = minus_apart[rows, cols]
                for k in range(2):
                    b = 2 * s + k
                    high = jnp.concatenate([row_hi[b, :, cols]] * 4, axis=0) - col_hi[b, rows, :]
                    low = jnp.concatenate([row_lo[b, :, cols]] * 4, axis=0) - col_lo[b, rows, :]
                    show[b, rows, cols] = jnp.maximum(jnp.minimum(high + low, bound), minus_bound)
            return carry

        lax.fori_loop(0, HP // 64, step, 0)

    pl.semaphore_wait(barrier, 18)

    def remote(src, dst, send, recv, device):
        copy = pltpu.make_async_remote_copy(
            src_ref=src, dst_ref=dst, send_sem=send, recv_sem=recv, device_id=device, device_id_type=MESH
        )
        copy.start()
        return copy

    board_copy = remote(board.at[0], board.at[1], sem_board.at[0], sem_board.at[1], other_core)
    ag1a, ag1b = [], []
    for d in range(1, N):
        ag1a.append(remote(line_a.at[z], line_a.at[z], ag_send.at[0, d], ag_recv.at[0, d], on_z(d)))
        ag1b.append(remote(line_b.at[y], line_b.at[y], ag_send.at[1, d], ag_recv.at[1, d], on_y(d)))

    prepare(0)
    ag2 = []
    for copy in ag1a:
        copy.wait_recv()
    rows_a[y] = line_a[...].reshape(16, SPLIT)
    for d in range(1, N):
        ag2.append(remote(rows_a.at[y], rows_a.at[y], ag_send.at[2, d], ag_recv.at[2, d], on_y(d)))
    for copy in ag1b:
        copy.wait_recv()
    rows_b[z] = line_b[...].reshape(16, HP - SPLIT)
    for d in range(1, N):
        ag2.append(remote(rows_b.at[z], rows_b.at[z], ag_send.at[3, d], ag_recv.at[3, d], on_z(d)))

    generate(0)
    board_copy.wait_recv()
    prepare(1)
    generate(1)

    for copy in ag2:
        copy.wait_recv()

    out_row = lax.broadcasted_iota(jnp.int32, (128, 128), 0)
    in_row = lax.broadcasted_iota(jnp.int32, (128, 128), 1)
    swapped = 16 * ((out_row // 2) % 8) + 2 * (out_row // 16) + out_row % 2
    swap = jnp.where(in_row == swapped, 1.0, 0.0).astype(BF16)
    own_a = rows_a[...].reshape(128, SPLIT)
    own_b = rows_b[...].reshape(128, HP - SPLIT)
    raw[1, :, 0:SPLIT] = own_a
    raw[0, :, SPLIT:HP] = own_b
    raw[0, :, 0:SPLIT] = jnp.dot(swap, own_a, preferred_element_type=F32).astype(BF16)
    raw[1, :, SPLIT:HP] = jnp.dot(swap, own_b, preferred_element_type=F32).astype(BF16)

    tail_lane = lax.broadcasted_iota(jnp.int32, (16, LANES), 1)

    def build(i, carry):
        rows = pl.ds(pl.multiple_of(i * 16, 16), 16)
        for o in range(2):
            tail = jnp.where(tail_lane == FLAG_LANE, raw[o, rows, TAIL:HP].astype(F32), 0.0)
            flag = jnp.broadcast_to(jnp.sum(tail, axis=1, keepdims=True), (16, LANES)).astype(BF16)
            for b in range(4):
                kept = keep[o, b, rows, :]
                shown = kept * flag
                folded = kept - shown
                fold_rows = pl.ds(pl.multiple_of(b * 128 + i * 16, 16), 16)
                for j in range(TILES):
                    cols = slice(j * LANES, (j + 1) * LANES)
                    masked = raw[o, rows, cols] * row_lv[b, :, cols]
                    lhs_show[o, b, rows, cols] = masked * shown
                    lhs_fold[o, fold_rows, cols] = masked * folded
        return carry

    lax.fori_loop(0, N, build, 0)

    part_lane = lax.broadcasted_iota(jnp.int32, (128, 256), 1)

    def card_sums(o):
        for b in range(4):
            rows = slice(b * 128, (b + 1) * 128)
            whole = jnp.dot(lhs_fold[o, rows, :], cards_left[...], preferred_element_type=F32)
            top = whole.astype(BF16).astype(F32)
            rest = whole - top
            middle = rest.astype(BF16).astype(F32)
            split = jnp.where(part_lane < PARTS[1], top, jnp.where(part_lane < PARTS[2], middle, rest - middle))
            sums[o, rows, :] = split.astype(BF16)

    rs1 = []
    for n, (o, first, width) in enumerate(CHUNKS):
        cols = slice(first, first + width)
        if n < 2:
            card_sums(o)
        folded = jnp.dot(sums[o], cards_right[:, cols], preferred_element_type=F32)
        total = jnp.zeros((128, width), F32)
        for b in range(4):
            shown = jnp.dot(lhs_show[o, b], show[b, :, cols], preferred_element_type=F32)
            own = lhs_fold[o, b * 128 : (b + 1) * 128, cols].astype(F32)
            total += ((folded[b * 128 : (b + 1) * 128] + own) + shown) * board[b // 2, 4 + b % 2 : 5 + b % 2, cols]
        part[n, :, 0:width] = total
        copies = []
        for d in range(1, N):
            target = z_peer(d) if o == 0 else y_peer(d)
            src = part.at[n, pl.ds(pl.multiple_of(target * 16, 16), 16), 0:width]
            copies.append(
                remote(src, recv1.at[n, d, :, 0:width], rs1_send.at[n, d], rs1_recv.at[n, d], on_z(d) if o == 0 else on_y(d))
            )
        rs1.append(copies)

    rs2 = []
    for n, (o, first, width) in enumerate(CHUNKS):
        mine = z if o == 0 else y
        total = part[n, pl.ds(pl.multiple_of(mine * 16, 16), 16), 0:width]
        for d in range(1, N):
            rs1[n][d - 1].wait_recv()
        for d in range(1, N):
            total += recv1[n, d, :, 0:width]
        for q in range(N):
            mid[q, :, first : first + width] = total[2 * q : 2 * q + 2]
        if n >= len(CHUNKS) - 2:
            cols = slice(0, SPLIT) if o == 0 else slice(SPLIT, HP)
            for d in range(1, N):
                target = y_peer(d) if o == 0 else z_peer(d)
                rs2.append(
                    remote(
                        mid.at[target, :, cols], recv2.at[d, :, cols], rs2_send.at[o, d], rs2_recv.at[o, d],
                        on_y(d) if o == 0 else on_z(d),
                    )
                )
    for copy in rs2:
        copy.wait_recv()
    value_a = mid[y, :, 0:SPLIT]
    value_b = mid[z, :, SPLIT:H]
    for d in range(1, N):
        value_a += recv2[d, :, 0:SPLIT]
        value_b += recv2[d, :, SPLIT:H]
    row_id = lax.broadcasted_iota(jnp.int32, (2, LANES), 0)
    pots = [pot[0, a].astype(F32) for a in range(2)]
    coefs = [jnp.where(kind[0, a] == 1, -pots[a], pots[a]) * (1.0 / (BOARDS * H)) for a in range(2)]
    coef = jnp.where(row_id == 0, coefs[0], coefs[1])[:, 0:1]
    for first, last, value in ((0, SPLIT, value_a), (SPLIT, H, value_b)):
        worth = value * coef
        held_regret = regrets[:, first:last]
        positive = jnp.maximum(held_regret, 0.0)
        strategy = (positive + FLOOR) / (jnp.sum(positive, axis=0, keepdims=True) + 2 * FLOOR)
        decision = jnp.sum(strategy * worth, axis=0, keepdims=True)
        new_regrets[:, first:last] = jnp.maximum(held_regret + worth - decision, 0.0)
        node[f, :, first:last] = decision

    flops = []
    for d in range(1, 4):
        own = node.at[f]
        flops.append(remote(own, own, fl_send.at[d], fl_recv.at[d], (lax.rem(f + d, 4), t, z)))
    for copy in flops:
        copy.wait_recv()
    chance[...] = ((node[0] + node[1]) + (node[2] + node[3])) * 0.25

    board_copy.wait_send()
    for copy in ag1a + ag1b + ag2 + rs2 + flops:
        copy.wait_send()
    for copies in rs1:
        for copy in copies:
            copy.wait_send()


def on_device(regrets, opp_reach, pot_size, line_kind, board_lines, board_count, hand_ranks, live_hands):
    vmem = pl.BlockSpec(memory_space=pltpu.VMEM)
    hbm = pl.BlockSpec(memory_space=pltpu.HBM)
    dma = pltpu.SemaphoreType.DMA
    left, right = card_tables()
    updated, chance = pl.pallas_call(
        kernel,
        out_shape=(jax.ShapeDtypeStruct((2, H), F32), jax.ShapeDtypeStruct((1, H), F32)),
        in_specs=[hbm] * 10,
        out_specs=(vmem, vmem),
        scratch_shapes=[
            pltpu.VMEM((2, H), F32),
            pltpu.VMEM((2, H), BF16),
            pltpu.SMEM((1, 2), jnp.int32),
            pltpu.SMEM((1, 2), jnp.int32),
            pltpu.VMEM((2, 256), jnp.int32),
            pltpu.SMEM((1, 2), jnp.int32),
            pltpu.VMEM((2, H), jnp.int32),
            pltpu.VMEM((2, H), jnp.int32),
            pltpu.VMEM((HP, 256), BF16),
            pltpu.VMEM((256, HP), BF16),
            pltpu.VMEM((HP, HP), BF16),
            pltpu.VMEM((HP, HP), BF16),
            pltpu.VMEM((4, HP, HP), BF16),
            pltpu.VMEM((N, 2, SPLIT), BF16),
            pltpu.VMEM((N, 2, HP - SPLIT), BF16),
            pltpu.VMEM((N, 16, SPLIT), BF16),
            pltpu.VMEM((N, 16, HP - SPLIT), BF16),
            pltpu.VMEM((2, 8, HP), F32),
            pltpu.VMEM((4, HP, LANES), BF16),
            pltpu.VMEM((4, HP, LANES), BF16),
            pltpu.VMEM((4, 16, HP), BF16),
            pltpu.VMEM((4, 16, HP), BF16),
            pltpu.VMEM((4, 16, HP), BF16),
            pltpu.VMEM((2, 4, 128, LANES), BF16),
            pltpu.VMEM((2, 128, HP), BF16),
            pltpu.VMEM((2, 4, 128, HP), BF16),
            pltpu.VMEM((2, 512, HP), BF16),
            pltpu.VMEM((2, 512, 256), BF16),
            pltpu.VMEM((6, 128, 256), F32),
            pltpu.VMEM((6, N, 16, 256), F32),
            pltpu.VMEM((N, 2, HP), F32),
            pltpu.VMEM((N, 2, HP), F32),
            pltpu.VMEM((4, 1, H), F32),
            dma((10,)),
            dma((2,)),
            dma((4, N)),
            dma((4, N)),
            dma((6, N)),
            dma((6, N)),
            dma((2, N)),
            dma((2, N)),
            dma((4,)),
            dma((4,)),
        ],
        compiler_params=pltpu.CompilerParams(
            collective_id=0, has_side_effects=True, vmem_limit_bytes=63 * 1024 * 1024
        ),
    )(
        regrets[0], opp_reach[0], pot_size, line_kind, board_lines[0, 0], board_count[0],
        hand_ranks[0, 0], live_hands[0, 0], jnp.asarray(left), jnp.asarray(right),
    )
    return updated[None], chance


def solution(mesh):
    lines = ("turn", "river")
    placed = (
        P("flop", lines, None),
        P("flop", lines, None),
        P("flop", lines),
        P("flop", lines),
        P("flop", "turn", "river", None),
        P("flop", "turn", "river"),
        P("flop", "turn", "river", None),
        P("flop", "turn", "river", None),
    )
    return jax.shard_map(
        on_device,
        mesh=mesh,
        in_specs=placed,
        out_specs=(P("flop", lines, None), P(lines, None)),
        check_vma=False,
    )
```

```python
import functools

import jax
import jax.numpy as jnp
import numpy as np
from jax import lax
from jax.experimental import pallas as pl
from jax.experimental.pallas import tpu as pltpu
from jax.sharding import PartitionSpec as P

CARDS = 52
H = 1326
LANES = 128
HP = 1408
TILES = HP // LANES
SPLIT = 768
TAIL = HP - LANES
FLAG_LANE = H - TAIL
BOARDS = 256
FLOOR = 0.1
N = 8
PARTS = (0, 128, 192)
MESH = pl.DeviceIdType.MESH
BF16 = jnp.bfloat16
F32 = jnp.float32

CHUNKS = ((0, 0, 256), (1, 768, 256), (0, 256, 256), (1, 1024, 256), (0, 512, 256), (1, 1280, 128))


def card_tables():
    first, second = np.triu_indices(CARDS, 1)
    hands = np.arange(H)
    left = np.zeros((HP, 256), np.float32)
    right = np.zeros((256, HP), np.float32)
    for start in PARTS:
        left[hands, start + first] = -1.0
        left[hands, start + second] = -1.0
        left[:, start + CARDS] = 1.0
        right[start + first, hands] = 1.0
        right[start + second, hands] = 1.0
        right[start + CARDS, :] = 1.0
    return left.astype(BF16), right.astype(BF16)


def kernel(*refs):
    sources, (new_regrets, chance), inputs, rest = refs[0:10], refs[10:12], refs[12:22], refs[22:]
    regrets, reach, pot, kind, lines, count, ranks, live, cards_left, cards_right = inputs
    (
        apart, minus_apart, show, line_a, line_b, rows_a, rows_b, board, col_hi, col_lo, row_hi, row_lo, row_lv,
        keep, raw, shows, lhs, sums,
        part_a, part_b, recv_a, recv_b, mid, recv2, node,
        sem_in, sem_board, ag_send, ag_recv, rs1_send, rs1_recv, rs2_send, rs2_recv, fl_sems,
    ) = rest
    f = lax.axis_index("flop")
    t = lax.axis_index("turn")
    z = lax.axis_index("river")
    y = t // 2
    c = t % 2

    def z_peer(d):
        return lax.rem(z + d, N)

    def y_peer(d):
        return lax.rem(y + d, N)

    def on_z(d):
        return (f, t, z_peer(d))

    def on_y(d):
        return (f, 2 * y_peer(d) + c, z)

    other_core = (f, 2 * y + (1 - c), z)

    loads = [pltpu.make_async_copy(sources[k], inputs[k], sem_in.at[k]) for k in range(10)]
    for load in loads:
        load.start()

    barrier = pltpu.get_barrier_semaphore()
    for d in range(1, N):
        pl.semaphore_signal(barrier, inc=1, device_id=on_z(d), device_id_type=MESH)
        pl.semaphore_signal(barrier, inc=1, device_id=on_y(d), device_id_type=MESH)
    pl.semaphore_signal(barrier, inc=1, device_id=other_core, device_id_type=MESH)
    for d in range(1, 4):
        pl.semaphore_signal(barrier, inc=1, device_id=(lax.rem(f + d, 4), t, z), device_id_type=MESH)

    for load in loads:
        load.wait()

    row_id = lax.broadcasted_iota(jnp.int32, (2, LANES), 0)
    lane_id = lax.broadcasted_iota(jnp.int32, (2, LANES), 1)
    flag0 = jnp.where(kind[0, 0] == 0, 1.0, 0.0).astype(F32)
    flag1 = jnp.where(kind[0, 1] == 0, 1.0, 0.0).astype(F32)
    flags = jnp.where(lane_id == FLAG_LANE, jnp.where(row_id == 0, flag0, flag1), 0.0)
    line_a[z] = reach[:, 0:SPLIT]
    line_b[y] = jnp.zeros((2, HP - SPLIT), BF16)
    line_b[y, :, 0 : H - SPLIT] = reach[:, SPLIT:H]
    tail = line_b[y, :, TAIL - SPLIT : HP - SPLIT].astype(F32)
    line_b[y, :, TAIL - SPLIT : HP - SPLIT] = (tail + flags).astype(BF16)

    board[0] = jnp.zeros((8, HP), F32)
    rank_high = (ranks[...] >> 7) << 7
    board[0, 0:2, 0:H] = rank_high.astype(F32)
    board[0, 2:4, 0:H] = (ranks[...] - rank_high).astype(F32)
    board[0, 4:6, 0:H] = live[...].astype(F32)
    slot_row = lax.broadcasted_iota(jnp.int32, (2, 256), 0)
    slot_id = lax.broadcasted_iota(jnp.int32, (2, 256), 1)
    limit = jnp.where(slot_row == 0, count[0, 0], count[0, 1])
    board[0, 6:8, 0:256] = jnp.where(slot_id < limit, lines[...], -1).astype(F32)

    def spread(i, carry):
        rows = pl.ds(pl.multiple_of(i * 128, 128), 128)
        for first, width in ((0, 512), (512, 512), (1024, 384)):
            cols = slice(first, first + width)
            free = jnp.dot(cards_left[rows, 0:128], cards_right[0:128, cols], preferred_element_type=F32)
            free = jnp.maximum(free, 0.0).astype(BF16)
            apart[rows, cols] = free
            minus_apart[rows, cols] = -free
        return carry

    lax.fori_loop(0, TILES, spread, 0)

    def prepare(s):
        for k in range(2):
            b = 2 * s + k
            for j in range(TILES):
                cols = slice(j * LANES, (j + 1) * LANES)
                col_hi[b, cols, :] = jnp.broadcast_to(board[s, k : k + 1, cols], (LANES, LANES)).T.astype(BF16)
                col_lo[b, cols, :] = jnp.broadcast_to(board[s, 2 + k : 3 + k, cols], (LANES, LANES)).T.astype(BF16)
            row_hi[b] = jnp.broadcast_to(board[s, k : k + 1, :], (16, HP)).astype(BF16)
            row_lo[b] = jnp.broadcast_to(board[s, 2 + k : 3 + k, :], (16, HP)).astype(BF16)
            row_lv[b] = jnp.broadcast_to(board[s, 4 + k : 5 + k, :], (16, HP)).astype(BF16)
            row = lax.broadcasted_iota(jnp.int32, (128, 256), 0)
            line = 32 * (row // 16) + 16 * c + row % 16
            slots = jnp.broadcast_to(board[s, 6 + k : 7 + k, 0:256], (128, 256))
            hit = jnp.where(slots == line.astype(F32), 1.0, 0.0)
            keep[b] = jnp.broadcast_to(jnp.sum(hit, axis=1, keepdims=True), (128, LANES)).astype(BF16)

    def generate(s):
        def step(i, carry):
            rows = pl.ds(pl.multiple_of(i * 64, 64), 64)
            for j in range(TILES):
                cols = slice(j * LANES, (j + 1) * LANES)
                bound = apart[rows, cols]
                minus_bound = minus_apart[rows, cols]
                for k in range(2):
                    b = 2 * s + k
                    high = jnp.concatenate([row_hi[b, :, cols]] * 4, axis=0) - col_hi[b, rows, :]
                    low = jnp.concatenate([row_lo[b, :, cols]] * 4, axis=0) - col_lo[b, rows, :]
                    show[b, rows, cols] = jnp.maximum(jnp.minimum(high + low, bound), minus_bound)
            return carry

        lax.fori_loop(0, HP // 64, step, 0)

    pl.semaphore_wait(barrier, 18)

    def remote(src, dst, send, recv, device):
        copy = pltpu.make_async_remote_copy(
            src_ref=src, dst_ref=dst, send_sem=send, recv_sem=recv, device_id=device, device_id_type=MESH
        )
        copy.start()

    def arrived(sem, ref):
        pltpu.make_async_copy(ref, ref, sem).wait()

    remote(board.at[0], board.at[1], sem_board.at[0], sem_board.at[1], other_core)
    for d in range(1, N):
        remote(line_a.at[z], line_a.at[z], ag_send.at[0], ag_recv.at[0], on_z(d))
        remote(line_b.at[y], line_b.at[y], ag_send.at[1], ag_recv.at[1], on_y(d))

    prepare(0)
    arrived(ag_recv.at[0], line_a.at[0 : N - 1])
    rows_a[y] = line_a[...].reshape(16, SPLIT)
    for d in range(1, N):
        remote(rows_a.at[y], rows_a.at[y], ag_send.at[2], ag_recv.at[2], on_y(d))
    arrived(ag_recv.at[1], line_b.at[0 : N - 1])
    rows_b[z] = line_b[...].reshape(16, HP - SPLIT)
    for d in range(1, N):
        remote(rows_b.at[z], rows_b.at[z], ag_send.at[3], ag_recv.at[3], on_z(d))

    generate(0)
    arrived(sem_board.at[1], board.at[1])
    prepare(1)
    generate(1)

    arrived(ag_recv.at[2], rows_a.at[0 : N - 1])
    arrived(ag_recv.at[3], rows_b.at[0 : N - 1])

    out_row = lax.broadcasted_iota(jnp.int32, (128, 128), 0)
    in_row = lax.broadcasted_iota(jnp.int32, (128, 128), 1)
    swapped = 16 * ((out_row // 2) % 8) + 2 * (out_row // 16) + out_row % 2
    swap = jnp.where(in_row == swapped, 1.0, 0.0).astype(BF16)
    raw[:, 0:SPLIT] = rows_a[...].reshape(128, SPLIT)
    raw[:, SPLIT:HP] = jnp.dot(swap, rows_b[...].reshape(128, HP - SPLIT), preferred_element_type=F32).astype(BF16)
    tail_lane = lax.broadcasted_iota(jnp.int32, (128, LANES), 1)
    tail = jnp.where(tail_lane == FLAG_LANE, raw[:, TAIL:HP].astype(F32), 0.0)
    shows[...] = jnp.broadcast_to(jnp.sum(tail, axis=1, keepdims=True), (128, 256))

    def build(i, carry):
        rows = pl.ds(pl.multiple_of(i * 16, 16), 16)
        for b in range(4):
            kept = keep[b, rows, :]
            for j in range(TILES):
                cols = slice(j * LANES, (j + 1) * LANES)
                lhs[b, rows, cols] = raw[rows, cols] * kept * row_lv[b, :, cols]
        return carry

    lax.fori_loop(0, N, build, 0)

    part_lane = lax.broadcasted_iota(jnp.int32, (128, 256), 1)

    for b in range(4):
        whole = jnp.dot(lhs[b], cards_left[...], preferred_element_type=F32)
        top = whole.astype(BF16).astype(F32)
        rest = whole - top
        middle = rest.astype(BF16).astype(F32)
        split = jnp.where(part_lane < PARTS[1], top, jnp.where(part_lane < PARTS[2], middle, rest - middle))
        sums[b * 128 : (b + 1) * 128, :] = split.astype(BF16)

    for n, (o, first, width) in enumerate(CHUNKS):
        cols = slice(first, first + width)
        m = n // 2
        folded = jnp.dot(sums[...], cards_right[:, cols], preferred_element_type=F32)
        is_show = shows[:, 0:width] > 0.5
        total = jnp.zeros((128, width), F32)
        for b in range(4):
            shown = jnp.dot(lhs[b], show[b, :, cols], preferred_element_type=F32)
            fold = folded[b * 128 : (b + 1) * 128] + lhs[b, :, cols].astype(F32)
            total += jnp.where(is_show, shown, fold) * board[b // 2, 4 + b % 2 : 5 + b % 2, cols]
        if o == 0:
            part_a[m] = total.reshape(N, N, 2, width)
        else:
            part_b[m, :, 0:width] = total
        for d in range(1, N):
            if o == 0:
                src, dst, device = part_a.at[m, :, z_peer(d)], recv_a.at[m, d], on_z(d)
            else:
                src = part_b.at[m, pl.ds(pl.multiple_of(y_peer(d) * 16, 16), 16), 0:width]
                dst, device = recv_b.at[m, d, :, 0:width], on_y(d)
            remote(src, dst, rs1_send.at[n], rs1_recv.at[n], device)

    def landed(n):
        o, first, width = CHUNKS[n]
        return recv_a.at[n // 2, 1:N] if o == 0 else recv_b.at[n // 2, 1:N, :, 0:width]

    halves = (slice(0, SPLIT), slice(SPLIT, HP))
    for n, (o, first, width) in enumerate(CHUNKS):
        cols = slice(first, first + width)
        m = n // 2
        arrived(rs1_recv.at[n], landed(n))
        if o == 0:
            total = part_a[m, :, z]
            for d in range(1, N):
                total += recv_a[m, d]
            mid[:, :, cols] = total
        else:
            total = part_b[m, pl.ds(pl.multiple_of(y * 16, 16), 16), 0:width]
            for d in range(1, N):
                total += recv_b[m, d, :, 0:width]
            for q in range(N):
                mid[q, :, cols] = total[2 * q : 2 * q + 2]
        if n >= len(CHUNKS) - 2:
            whole = halves[o]
            for d in range(1, N):
                target, device = (y_peer(d), on_y(d)) if o == 0 else (z_peer(d), on_z(d))
                remote(mid.at[target, :, whole], recv2.at[d, :, whole], rs2_send.at[o], rs2_recv.at[o], device)
    arrived(rs2_recv.at[0], recv2.at[1:N, :, halves[0]])
    arrived(rs2_recv.at[1], recv2.at[1:N, :, halves[1]])
    value_a = mid[y, :, 0:SPLIT]
    value_b = mid[z, :, SPLIT:H]
    for d in range(1, N):
        value_a += recv2[d, :, 0:SPLIT]
        value_b += recv2[d, :, SPLIT:H]
    row_id = lax.broadcasted_iota(jnp.int32, (2, LANES), 0)
    pots = [pot[0, a].astype(F32) for a in range(2)]
    coefs = [jnp.where(kind[0, a] == 1, -pots[a], pots[a]) * (1.0 / (BOARDS * H)) for a in range(2)]
    coef = jnp.where(row_id == 0, coefs[0], coefs[1])[:, 0:1]
    for first, last, value in ((0, SPLIT, value_a), (SPLIT, H, value_b)):
        worth = value * coef
        held_regret = regrets[:, first:last]
        positive = jnp.maximum(held_regret, 0.0)
        strategy = (positive + FLOOR) / (jnp.sum(positive, axis=0, keepdims=True) + 2 * FLOOR)
        decision = jnp.sum(strategy * worth, axis=0, keepdims=True)
        new_regrets[:, first:last] = jnp.maximum(held_regret + worth - decision, 0.0)
        node[f, :, first:last] = decision

    for d in range(1, 4):
        remote(node.at[f], node.at[f], fl_sems.at[0], fl_sems.at[1], (lax.rem(f + d, 4), t, z))
    arrived(fl_sems.at[1], node.at[0:3])
    chance[...] = ((node[0] + node[1]) + (node[2] + node[3])) * 0.25

    arrived(sem_board.at[0], board.at[0])
    arrived(ag_send.at[0], line_a.at[0 : N - 1])
    arrived(ag_send.at[1], line_b.at[0 : N - 1])
    arrived(ag_send.at[2], rows_a.at[0 : N - 1])
    arrived(ag_send.at[3], rows_b.at[0 : N - 1])
    for n in range(len(CHUNKS)):
        arrived(rs1_send.at[n], landed(n))
    for o in range(2):
        arrived(rs2_send.at[o], recv2.at[1:N, :, halves[o]])
    arrived(fl_sems.at[0], node.at[0:3])


def on_device(regrets, opp_reach, pot_size, line_kind, board_lines, board_count, hand_ranks, live_hands):
    vmem = pl.BlockSpec(memory_space=pltpu.VMEM)
    hbm = pl.BlockSpec(memory_space=pltpu.HBM)
    dma = pltpu.SemaphoreType.DMA
    left, right = card_tables()
    updated, chance = pl.pallas_call(
        kernel,
        out_shape=(jax.ShapeDtypeStruct((2, H), F32), jax.ShapeDtypeStruct((1, H), F32)),
        in_specs=[hbm] * 10,
        out_specs=(vmem, vmem),
        scratch_shapes=[
            pltpu.VMEM((2, H), F32),
            pltpu.VMEM((2, H), BF16),
            pltpu.SMEM((1, 2), jnp.int32),
            pltpu.SMEM((1, 2), jnp.int32),
            pltpu.VMEM((2, 256), jnp.int32),
            pltpu.SMEM((1, 2), jnp.int32),
            pltpu.VMEM((2, H), jnp.int32),
            pltpu.VMEM((2, H), jnp.int32),
            pltpu.VMEM((HP, 256), BF16),
            pltpu.VMEM((256, HP), BF16),
            pltpu.VMEM((HP, HP), BF16),
            pltpu.VMEM((HP, HP), BF16),
            pltpu.VMEM((4, HP, HP), BF16),
            pltpu.VMEM((N, 2, SPLIT), BF16),
            pltpu.VMEM((N, 2, HP - SPLIT), BF16),
            pltpu.VMEM((N, 16, SPLIT), BF16),
            pltpu.VMEM((N, 16, HP - SPLIT), BF16),
            pltpu.VMEM((2, 8, HP), F32),
            pltpu.VMEM((4, HP, LANES), BF16),
            pltpu.VMEM((4, HP, LANES), BF16),
            pltpu.VMEM((4, 16, HP), BF16),
            pltpu.VMEM((4, 16, HP), BF16),
            pltpu.VMEM((4, 16, HP), BF16),
            pltpu.VMEM((4, 128, LANES), BF16),
            pltpu.VMEM((128, HP), BF16),
            pltpu.VMEM((128, 256), F32),
            pltpu.VMEM((4, 128, HP), BF16),
            pltpu.VMEM((512, 256), BF16),
            pltpu.VMEM((3, N, N, 2, 256), F32),
            pltpu.VMEM((3, 128, 256), F32),
            pltpu.VMEM((3, N, N, 2, 256), F32),
            pltpu.VMEM((3, N, 16, 256), F32),
            pltpu.VMEM((N, 2, HP), F32),
            pltpu.VMEM((N, 2, HP), F32),
            pltpu.VMEM((4, 1, H), F32),
            dma((10,)),
            dma((2,)),
            dma((4,)),
            dma((4,)),
            dma((6,)),
            dma((6,)),
            dma((2,)),
            dma((2,)),
            dma((2,)),
        ],
        compiler_params=pltpu.CompilerParams(
            collective_id=0, has_side_effects=True, vmem_limit_bytes=63 * 1024 * 1024
        ),
    )(
        regrets[0], opp_reach[0], pot_size, line_kind, board_lines[0, 0], board_count[0],
        hand_ranks[0, 0], live_hands[0, 0], jnp.asarray(left), jnp.asarray(right),
    )
    return updated[None], chance


def solution(mesh):
    lines = ("turn", "river")
    placed = (
        P("flop", lines, None),
        P("flop", lines, None),
        P("flop", lines),
        P("flop", lines),
        P("flop", "turn", "river", None),
        P("flop", "turn", "river"),
        P("flop", "turn", "river", None),
        P("flop", "turn", "river", None),
    )
    return jax.shard_map(
        on_device,
        mesh=mesh,
        in_specs=placed,
        out_specs=(P("flop", lines, None), P(lines, None)),
        check_vma=False,
    )
```

```python
import functools

import jax
import jax.numpy as jnp
import numpy as np
from jax import lax
from jax.experimental import pallas as pl
from jax.experimental.pallas import tpu as pltpu
from jax.sharding import PartitionSpec as P

CARDS = 52
H = 1326
LANES = 128
HP = 1408
TILES = HP // LANES
SPLIT = 768
TAIL = HP - LANES
FLAG_LANE = H - TAIL
BOARDS = 256
FLOOR = 0.1
N = 8
PARTS = (0, 128, 192)
FAR = (4, 3, 5, 2, 6, 1, 7)
MESH = pl.DeviceIdType.MESH
BF16 = jnp.bfloat16
F32 = jnp.float32

CHUNKS = ((0, 0, 256), (1, 768, 256), (0, 256, 256), (1, 1024, 256), (0, 512, 256), (1, 1280, 128))


def card_tables():
    first, second = np.triu_indices(CARDS, 1)
    hands = np.arange(H)
    left = np.zeros((HP, 256), np.float32)
    right = np.zeros((256, HP), np.float32)
    for start in PARTS:
        left[hands, start + first] = -1.0
        left[hands, start + second] = -1.0
        left[:, start + CARDS] = 1.0
        right[start + first, hands] = 1.0
        right[start + second, hands] = 1.0
        right[start + CARDS, :] = 1.0
    return left.astype(BF16), right.astype(BF16)


def kernel(*refs):
    sources, (new_regrets, chance), inputs, rest = refs[0:10], refs[10:12], refs[12:22], refs[22:]
    regrets, reach, pot, kind, lines, count, ranks, live, cards_left, cards_right = inputs
    (
        apart, minus_apart, show, line_a, line_b, rows_a, rows_b, board, col_hi, col_lo, row_hi, row_lo, row_lv,
        keep, raw, shows, lhs, sums,
        part_a, part_b, recv_a, recv_b, mid, recv2, node,
        sem_in, sem_board, ag_send, ag_recv, rs1_send, rs1_recv, rs2_send, rs2_recv, fl_sems,
    ) = rest
    f = lax.axis_index("flop")
    t = lax.axis_index("turn")
    z = lax.axis_index("river")
    y = t // 2
    c = t % 2

    def z_peer(d):
        return lax.rem(z + d, N)

    def y_peer(d):
        return lax.rem(y + d, N)

    def on_z(d):
        return (f, t, z_peer(d))

    def on_y(d):
        return (f, 2 * y_peer(d) + c, z)

    other_core = (f, 2 * y + (1 - c), z)

    loads = [pltpu.make_async_copy(sources[k], inputs[k], sem_in.at[k]) for k in range(10)]
    for load in loads:
        load.start()

    barrier = pltpu.get_barrier_semaphore()
    for d in FAR:
        pl.semaphore_signal(barrier, inc=1, device_id=on_z(d), device_id_type=MESH)
        pl.semaphore_signal(barrier, inc=1, device_id=on_y(d), device_id_type=MESH)
    pl.semaphore_signal(barrier, inc=1, device_id=other_core, device_id_type=MESH)
    for d in (2, 1, 3):
        pl.semaphore_signal(barrier, inc=1, device_id=(lax.rem(f + d, 4), t, z), device_id_type=MESH)

    for load in loads:
        load.wait()

    row_id = lax.broadcasted_iota(jnp.int32, (2, LANES), 0)
    lane_id = lax.broadcasted_iota(jnp.int32, (2, LANES), 1)
    flag0 = jnp.where(kind[0, 0] == 0, 1.0, 0.0).astype(F32)
    flag1 = jnp.where(kind[0, 1] == 0, 1.0, 0.0).astype(F32)
    flags = jnp.where(lane_id == FLAG_LANE, jnp.where(row_id == 0, flag0, flag1), 0.0)
    line_a[z] = reach[:, 0:SPLIT]
    line_b[y] = jnp.zeros((2, HP - SPLIT), BF16)
    line_b[y, :, 0 : H - SPLIT] = reach[:, SPLIT:H]
    tail = line_b[y, :, TAIL - SPLIT : HP - SPLIT].astype(F32)
    line_b[y, :, TAIL - SPLIT : HP - SPLIT] = (tail + flags).astype(BF16)

    board[0] = jnp.zeros((8, HP), F32)
    rank_high = (ranks[...] >> 7) << 7
    board[0, 0:2, 0:H] = rank_high.astype(F32)
    board[0, 2:4, 0:H] = (ranks[...] - rank_high).astype(F32)
    board[0, 4:6, 0:H] = live[...].astype(F32)
    slot_row = lax.broadcasted_iota(jnp.int32, (2, 256), 0)
    slot_id = lax.broadcasted_iota(jnp.int32, (2, 256), 1)
    limit = jnp.where(slot_row == 0, count[0, 0], count[0, 1])
    board[0, 6:8, 0:256] = jnp.where(slot_id < limit, lines[...], -1).astype(F32)

    def spread(i, carry):
        rows = pl.ds(pl.multiple_of(i * 128, 128), 128)
        for first, width in ((0, 512), (512, 512), (1024, 384)):
            cols = slice(first, first + width)
            free = jnp.dot(cards_left[rows, 0:128], cards_right[0:128, cols], preferred_element_type=F32)
            free = jnp.maximum(free, 0.0).astype(BF16)
            apart[rows, cols] = free
            minus_apart[rows, cols] = -free
        return carry


    def prepare(s):
        for k in range(2):
            b = 2 * s + k
            for j in range(TILES):
                cols = slice(j * LANES, (j + 1) * LANES)
                col_hi[b, cols, :] = jnp.broadcast_to(board[s, k : k + 1, cols], (LANES, LANES)).T.astype(BF16)
                col_lo[b, cols, :] = jnp.broadcast_to(board[s, 2 + k : 3 + k, cols], (LANES, LANES)).T.astype(BF16)
            row_hi[b] = jnp.broadcast_to(board[s, k : k + 1, :], (16, HP)).astype(BF16)
            row_lo[b] = jnp.broadcast_to(board[s, 2 + k : 3 + k, :], (16, HP)).astype(BF16)
            row_lv[b] = jnp.broadcast_to(board[s, 4 + k : 5 + k, :], (16, HP)).astype(BF16)
            row = lax.broadcasted_iota(jnp.int32, (128, 256), 0)
            line = 32 * (row // 16) + 16 * c + row % 16
            slots = jnp.broadcast_to(board[s, 6 + k : 7 + k, 0:256], (128, 256))
            hit = jnp.where(slots == line.astype(F32), 1.0, 0.0)
            keep[b] = jnp.broadcast_to(jnp.sum(hit, axis=1, keepdims=True), (128, LANES)).astype(BF16)

    def generate(s):
        def step(i, carry):
            rows = pl.ds(pl.multiple_of(i * 64, 64), 64)
            for j in range(TILES):
                cols = slice(j * LANES, (j + 1) * LANES)
                bound = apart[rows, cols]
                minus_bound = minus_apart[rows, cols]
                for k in range(2):
                    b = 2 * s + k
                    high = jnp.concatenate([row_hi[b, :, cols]] * 4, axis=0) - col_hi[b, rows, :]
                    low = jnp.concatenate([row_lo[b, :, cols]] * 4, axis=0) - col_lo[b, rows, :]
                    show[b, rows, cols] = jnp.maximum(jnp.minimum(high + low, bound), minus_bound)
            return carry

        lax.fori_loop(0, HP // 64, step, 0)

    pl.semaphore_wait(barrier, 18)

    def remote(src, dst, send, recv, device):
        copy = pltpu.make_async_remote_copy(
            src_ref=src, dst_ref=dst, send_sem=send, recv_sem=recv, device_id=device, device_id_type=MESH
        )
        copy.start()

    def arrived(sem, ref):
        pltpu.make_async_copy(ref, ref, sem).wait()

    remote(board.at[0], board.at[1], sem_board.at[0], sem_board.at[1], other_core)
    for d in FAR:
        remote(line_a.at[z], line_a.at[z], ag_send.at[0], ag_recv.at[0], on_z(d))
        remote(line_b.at[y], line_b.at[y], ag_send.at[1], ag_recv.at[1], on_y(d))

    lax.fori_loop(0, TILES, spread, 0)
    prepare(0)
    arrived(ag_recv.at[0], line_a.at[0 : N - 1])
    rows_a[y] = line_a[...].reshape(16, SPLIT)
    for d in FAR:
        remote(rows_a.at[y], rows_a.at[y], ag_send.at[2], ag_recv.at[2], on_y(d))
    arrived(ag_recv.at[1], line_b.at[0 : N - 1])
    rows_b[z] = line_b[...].reshape(16, HP - SPLIT)
    for d in FAR:
        remote(rows_b.at[z], rows_b.at[z], ag_send.at[3], ag_recv.at[3], on_z(d))

    generate(0)
    arrived(sem_board.at[1], board.at[1])
    prepare(1)
    generate(1)

    arrived(ag_recv.at[2], rows_a.at[0 : N - 1])
    arrived(ag_recv.at[3], rows_b.at[0 : N - 1])

    out_row = lax.broadcasted_iota(jnp.int32, (128, 128), 0)
    in_row = lax.broadcasted_iota(jnp.int32, (128, 128), 1)
    swapped = 16 * ((out_row // 2) % 8) + 2 * (out_row // 16) + out_row % 2
    swap = jnp.where(in_row == swapped, 1.0, 0.0).astype(BF16)
    raw[:, 0:SPLIT] = rows_a[...].reshape(128, SPLIT)
    raw[:, SPLIT:HP] = jnp.dot(swap, rows_b[...].reshape(128, HP - SPLIT), preferred_element_type=F32).astype(BF16)
    tail_lane = lax.broadcasted_iota(jnp.int32, (128, LANES), 1)
    tail = jnp.where(tail_lane == FLAG_LANE, raw[:, TAIL:HP].astype(F32), 0.0)
    shows[...] = jnp.broadcast_to(jnp.sum(tail, axis=1, keepdims=True), (128, 256))

    def build(i, carry):
        rows = pl.ds(pl.multiple_of(i * 16, 16), 16)
        for b in range(4):
            kept = keep[b, rows, :]
            for j in range(TILES):
                cols = slice(j * LANES, (j + 1) * LANES)
                lhs[b, rows, cols] = raw[rows, cols] * kept * row_lv[b, :, cols]
        return carry

    lax.fori_loop(0, N, build, 0)

    part_lane = lax.broadcasted_iota(jnp.int32, (128, 256), 1)

    for b in range(4):
        whole = jnp.dot(lhs[b], cards_left[...], preferred_element_type=F32)
        top = whole.astype(BF16).astype(F32)
        rest = whole - top
        middle = rest.astype(BF16).astype(F32)
        split = jnp.where(part_lane < PARTS[1], top, jnp.where(part_lane < PARTS[2], middle, rest - middle))
        sums[b * 128 : (b + 1) * 128, :] = split.astype(BF16)

    for n, (o, first, width) in enumerate(CHUNKS):
        cols = slice(first, first + width)
        m = n // 2
        folded = jnp.dot(sums[...], cards_right[:, cols], preferred_element_type=F32)
        is_show = shows[:, 0:width] > 0.5
        total = jnp.zeros((128, width), F32)
        for b in range(4):
            shown = jnp.dot(lhs[b], show[b, :, cols], preferred_element_type=F32)
            fold = folded[b * 128 : (b + 1) * 128] + lhs[b, :, cols].astype(F32)
            total += jnp.where(is_show, shown, fold) * board[b // 2, 4 + b % 2 : 5 + b % 2, cols]
        if o == 0:
            part_a[m] = total.reshape(N, N, 2, width)
        else:
            part_b[m, :, 0:width] = total
        for d in FAR:
            if o == 0:
                src, dst, device = part_a.at[m, :, z_peer(d)], recv_a.at[m, d], on_z(d)
            else:
                src = part_b.at[m, pl.ds(pl.multiple_of(y_peer(d) * 16, 16), 16), 0:width]
                dst, device = recv_b.at[m, d, :, 0:width], on_y(d)
            remote(src, dst, rs1_send.at[n], rs1_recv.at[n], device)

    def landed(n):
        o, first, width = CHUNKS[n]
        return recv_a.at[n // 2, 1:N] if o == 0 else recv_b.at[n // 2, 1:N, :, 0:width]

    halves = (slice(0, SPLIT), slice(SPLIT, HP))
    for n, (o, first, width) in enumerate(CHUNKS):
        cols = slice(first, first + width)
        m = n // 2
        arrived(rs1_recv.at[n], landed(n))
        if o == 0:
            total = part_a[m, :, z]
            for d in FAR:
                total += recv_a[m, d]
            mid[:, :, cols] = total
        else:
            total = part_b[m, pl.ds(pl.multiple_of(y * 16, 16), 16), 0:width]
            for d in FAR:
                total += recv_b[m, d, :, 0:width]
            for q in range(N):
                mid[q, :, cols] = total[2 * q : 2 * q + 2]
        if n >= len(CHUNKS) - 2:
            whole = halves[o]
            for d in FAR:
                target, device = (y_peer(d), on_y(d)) if o == 0 else (z_peer(d), on_z(d))
                remote(mid.at[target, :, whole], recv2.at[d, :, whole], rs2_send.at[o], rs2_recv.at[o], device)
    arrived(rs2_recv.at[0], recv2.at[1:N, :, halves[0]])
    arrived(rs2_recv.at[1], recv2.at[1:N, :, halves[1]])
    value_a = mid[y, :, 0:SPLIT]
    value_b = mid[z, :, SPLIT:H]
    for d in FAR:
        value_a += recv2[d, :, 0:SPLIT]
        value_b += recv2[d, :, SPLIT:H]
    row_id = lax.broadcasted_iota(jnp.int32, (2, LANES), 0)
    pots = [pot[0, a].astype(F32) for a in range(2)]
    coefs = [jnp.where(kind[0, a] == 1, -pots[a], pots[a]) * (1.0 / (BOARDS * H)) for a in range(2)]
    coef = jnp.where(row_id == 0, coefs[0], coefs[1])[:, 0:1]
    for first, last, value in ((0, SPLIT, value_a), (SPLIT, H, value_b)):
        worth = value * coef
        held_regret = regrets[:, first:last]
        positive = jnp.maximum(held_regret, 0.0)
        strategy = (positive + FLOOR) / (jnp.sum(positive, axis=0, keepdims=True) + 2 * FLOOR)
        decision = jnp.sum(strategy * worth, axis=0, keepdims=True)
        new_regrets[:, first:last] = jnp.maximum(held_regret + worth - decision, 0.0)
        node[f, :, first:last] = decision

    for d in (2, 1, 3):
        remote(node.at[f], node.at[f], fl_sems.at[0], fl_sems.at[1], (lax.rem(f + d, 4), t, z))
    arrived(fl_sems.at[1], node.at[0:3])
    chance[...] = ((node[0] + node[1]) + (node[2] + node[3])) * 0.25

    arrived(sem_board.at[0], board.at[0])
    arrived(ag_send.at[0], line_a.at[0 : N - 1])
    arrived(ag_send.at[1], line_b.at[0 : N - 1])
    arrived(ag_send.at[2], rows_a.at[0 : N - 1])
    arrived(ag_send.at[3], rows_b.at[0 : N - 1])
    for n in range(len(CHUNKS)):
        arrived(rs1_send.at[n], landed(n))
    for o in range(2):
        arrived(rs2_send.at[o], recv2.at[1:N, :, halves[o]])
    arrived(fl_sems.at[0], node.at[0:3])


def on_device(regrets, opp_reach, pot_size, line_kind, board_lines, board_count, hand_ranks, live_hands):
    vmem = pl.BlockSpec(memory_space=pltpu.VMEM)
    hbm = pl.BlockSpec(memory_space=pltpu.HBM)
    dma = pltpu.SemaphoreType.DMA
    left, right = card_tables()
    updated, chance = pl.pallas_call(
        kernel,
        out_shape=(jax.ShapeDtypeStruct((2, H), F32), jax.ShapeDtypeStruct((1, H), F32)),
        in_specs=[hbm] * 10,
        out_specs=(vmem, vmem),
        scratch_shapes=[
            pltpu.VMEM((2, H), F32),
            pltpu.VMEM((2, H), BF16),
            pltpu.SMEM((1, 2), jnp.int32),
            pltpu.SMEM((1, 2), jnp.int32),
            pltpu.VMEM((2, 256), jnp.int32),
            pltpu.SMEM((1, 2), jnp.int32),
            pltpu.VMEM((2, H), jnp.int32),
            pltpu.VMEM((2, H), jnp.int32),
            pltpu.VMEM((HP, 256), BF16),
            pltpu.VMEM((256, HP), BF16),
            pltpu.VMEM((HP, HP), BF16),
            pltpu.VMEM((HP, HP), BF16),
            pltpu.VMEM((4, HP, HP), BF16),
            pltpu.VMEM((N, 2, SPLIT), BF16),
            pltpu.VMEM((N, 2, HP - SPLIT), BF16),
            pltpu.VMEM((N, 16, SPLIT), BF16),
            pltpu.VMEM((N, 16, HP - SPLIT), BF16),
            pltpu.VMEM((2, 8, HP), F32),
            pltpu.VMEM((4, HP, LANES), BF16),
            pltpu.VMEM((4, HP, LANES), BF16),
            pltpu.VMEM((4, 16, HP), BF16),
            pltpu.VMEM((4, 16, HP), BF16),
            pltpu.VMEM((4, 16, HP), BF16),
            pltpu.VMEM((4, 128, LANES), BF16),
            pltpu.VMEM((128, HP), BF16),
            pltpu.VMEM((128, 256), F32),
            pltpu.VMEM((4, 128, HP), BF16),
            pltpu.VMEM((512, 256), BF16),
            pltpu.VMEM((3, N, N, 2, 256), F32),
            pltpu.VMEM((3, 128, 256), F32),
            pltpu.VMEM((3, N, N, 2, 256), F32),
            pltpu.VMEM((3, N, 16, 256), F32),
            pltpu.VMEM((N, 2, HP), F32),
            pltpu.VMEM((N, 2, HP), F32),
            pltpu.VMEM((4, 1, H), F32),
            dma((10,)),
            dma((2,)),
            dma((4,)),
            dma((4,)),
            dma((6,)),
            dma((6,)),
            dma((2,)),
            dma((2,)),
            dma((2,)),
        ],
        compiler_params=pltpu.CompilerParams(
            collective_id=0, has_side_effects=True, vmem_limit_bytes=48 * 1024 * 1024
        ),
    )(
        *(
            pltpu.with_memory_space_constraint(array, pltpu.HBM)
            for array in (
                regrets[0], opp_reach[0], pot_size, line_kind, board_lines[0, 0], board_count[0],
                hand_ranks[0, 0], live_hands[0, 0], jnp.asarray(left), jnp.asarray(right),
            )
        )
    )
    return updated[None], chance


def solution(mesh):
    lines = ("turn", "river")
    placed = (
        P("flop", lines, None),
        P("flop", lines, None),
        P("flop", lines),
        P("flop", lines),
        P("flop", "turn", "river", None),
        P("flop", "turn", "river"),
        P("flop", "turn", "river", None),
        P("flop", "turn", "river", None),
    )
    return jax.shard_map(
        on_device,
        mesh=mesh,
        in_specs=placed,
        out_specs=(P("flop", lines, None), P(lines, None)),
        check_vma=False,
    )
```

```python
import functools

import jax
import jax.numpy as jnp
import numpy as np
from jax import lax
from jax.experimental import pallas as pl
from jax.experimental.pallas import tpu as pltpu
from jax.sharding import PartitionSpec as P

CARDS = 52
H = 1326
LANES = 128
HP = 1408
TILES = HP // LANES
SPLIT = 768
TAIL = HP - LANES
FLAG_LANE = H - TAIL
BOARDS = 256
FLOOR = 0.1
N = 8
PARTS = (0, 128, 192)
FAR = (4, 5, 3, 6, 2, 7, 1)
MESH = pl.DeviceIdType.MESH
BF16 = jnp.bfloat16
F32 = jnp.float32

CHUNKS = ((0, 0, 256), (1, 768, 256), (0, 256, 256), (1, 1024, 256), (0, 512, 256), (1, 1280, 128))


def card_tables():
    first, second = np.triu_indices(CARDS, 1)
    hands = np.arange(H)
    left = np.zeros((HP, 256), np.float32)
    right = np.zeros((256, HP), np.float32)
    for start in PARTS:
        left[hands, start + first] = -1.0
        left[hands, start + second] = -1.0
        left[:, start + CARDS] = 1.0
        right[start + first, hands] = 1.0
        right[start + second, hands] = 1.0
        right[start + CARDS, :] = 1.0
    return left.astype(BF16), right.astype(BF16)


def kernel(*refs):
    sources, (new_regrets, chance), inputs, rest = refs[0:10], refs[10:12], refs[12:22], refs[22:]
    regrets, reach, pot, kind, lines, count, ranks, live, cards_left, cards_right = inputs
    (
        apart, minus_apart, show, line_a, line_b, rows_a, rows_b, board, col_hi, col_lo, row_hi, row_lo, row_lv,
        keep, raw, shows, lhs, sums,
        part_a, part_b, recv_a, recv_b, mid, recv2, node,
        sem_in, sem_board, ag_send, ag_recv, rs1_send, rs1_recv, rs2_send, rs2_recv, fl_sems,
    ) = rest
    f = lax.axis_index("flop")
    t = lax.axis_index("turn")
    z = lax.axis_index("river")
    y = t // 2
    c = t % 2

    def z_peer(d):
        return lax.rem(z + d, N)

    def y_peer(d):
        return lax.rem(y + d, N)

    def on_z(d):
        return (f, t, z_peer(d))

    def on_y(d):
        return (f, 2 * y_peer(d) + c, z)

    other_core = (f, 2 * y + (1 - c), z)

    loads = [pltpu.make_async_copy(sources[k], inputs[k], sem_in.at[k]) for k in range(10)]
    for load in loads:
        load.start()

    barrier = pltpu.get_barrier_semaphore()
    for d in FAR:
        pl.semaphore_signal(barrier, inc=1, device_id=on_z(d), device_id_type=MESH)
        pl.semaphore_signal(barrier, inc=1, device_id=on_y(d), device_id_type=MESH)
    pl.semaphore_signal(barrier, inc=1, device_id=other_core, device_id_type=MESH)
    for d in (2, 1, 3):
        pl.semaphore_signal(barrier, inc=1, device_id=(lax.rem(f + d, 4), t, z), device_id_type=MESH)

    for load in loads:
        load.wait()

    row_id = lax.broadcasted_iota(jnp.int32, (2, LANES), 0)
    lane_id = lax.broadcasted_iota(jnp.int32, (2, LANES), 1)
    flag0 = jnp.where(kind[0, 0] == 0, 1.0, 0.0).astype(F32)
    flag1 = jnp.where(kind[0, 1] == 0, 1.0, 0.0).astype(F32)
    flags = jnp.where(lane_id == FLAG_LANE, jnp.where(row_id == 0, flag0, flag1), 0.0)
    line_a[z] = reach[:, 0:SPLIT]
    line_b[y] = jnp.zeros((2, HP - SPLIT), BF16)
    line_b[y, :, 0 : H - SPLIT] = reach[:, SPLIT:H]
    tail = line_b[y, :, TAIL - SPLIT : HP - SPLIT].astype(F32)
    line_b[y, :, TAIL - SPLIT : HP - SPLIT] = (tail + flags).astype(BF16)

    board[0] = jnp.zeros((8, HP), F32)
    rank_high = (ranks[...] >> 7) << 7
    board[0, 0:2, 0:H] = rank_high.astype(F32)
    board[0, 2:4, 0:H] = (ranks[...] - rank_high).astype(F32)
    board[0, 4:6, 0:H] = live[...].astype(F32)
    slot_row = lax.broadcasted_iota(jnp.int32, (2, 256), 0)
    slot_id = lax.broadcasted_iota(jnp.int32, (2, 256), 1)
    limit = jnp.where(slot_row == 0, count[0, 0], count[0, 1])
    board[0, 6:8, 0:256] = jnp.where(slot_id < limit, lines[...], -1).astype(F32)

    def spread(i, carry):
        rows = pl.ds(pl.multiple_of(i * 128, 128), 128)
        for first, width in ((0, 512), (512, 512), (1024, 384)):
            cols = slice(first, first + width)
            free = jnp.dot(cards_left[rows, 0:128], cards_right[0:128, cols], preferred_element_type=F32)
            free = jnp.maximum(free, 0.0).astype(BF16)
            apart[rows, cols] = free
            minus_apart[rows, cols] = -free
        return carry


    def prepare(s):
        for k in range(2):
            b = 2 * s + k
            for j in range(TILES):
                cols = slice(j * LANES, (j + 1) * LANES)
                col_hi[b, cols, :] = jnp.broadcast_to(board[s, k : k + 1, cols], (LANES, LANES)).T.astype(BF16)
                col_lo[b, cols, :] = jnp.broadcast_to(board[s, 2 + k : 3 + k, cols], (LANES, LANES)).T.astype(BF16)
            row_hi[b] = jnp.broadcast_to(board[s, k : k + 1, :], (16, HP)).astype(BF16)
            row_lo[b] = jnp.broadcast_to(board[s, 2 + k : 3 + k, :], (16, HP)).astype(BF16)
            row_lv[b] = jnp.broadcast_to(board[s, 4 + k : 5 + k, :], (16, HP)).astype(BF16)
            row = lax.broadcasted_iota(jnp.int32, (128, 256), 0)
            line = 32 * (row // 16) + 16 * c + row % 16
            slots = jnp.broadcast_to(board[s, 6 + k : 7 + k, 0:256], (128, 256))
            hit = jnp.where(slots == line.astype(F32), 1.0, 0.0)
            keep[b] = jnp.broadcast_to(jnp.sum(hit, axis=1, keepdims=True), (128, LANES)).astype(BF16)

    def generate(s):
        def step(i, carry):
            rows = pl.ds(pl.multiple_of(i * 64, 64), 64)
            for j in range(TILES):
                cols = slice(j * LANES, (j + 1) * LANES)
                bound = apart[rows, cols]
                minus_bound = minus_apart[rows, cols]
                for k in range(2):
                    b = 2 * s + k
                    high = jnp.concatenate([row_hi[b, :, cols]] * 4, axis=0) - col_hi[b, rows, :]
                    low = jnp.concatenate([row_lo[b, :, cols]] * 4, axis=0) - col_lo[b, rows, :]
                    show[b, rows, cols] = jnp.maximum(jnp.minimum(high + low, bound), minus_bound)
            return carry

        lax.fori_loop(0, HP // 64, step, 0)

    pl.semaphore_wait(barrier, 18)

    def remote(src, dst, send, recv, device):
        copy = pltpu.make_async_remote_copy(
            src_ref=src, dst_ref=dst, send_sem=send, recv_sem=recv, device_id=device, device_id_type=MESH
        )
        copy.start()

    def arrived(sem, ref):
        pltpu.make_async_copy(ref, ref, sem).wait()

    remote(board.at[0], board.at[1], sem_board.at[0], sem_board.at[1], other_core)
    for d in FAR:
        remote(line_a.at[z], line_a.at[z], ag_send.at[0], ag_recv.at[0], on_z(d))
        remote(line_b.at[y], line_b.at[y], ag_send.at[1], ag_recv.at[1], on_y(d))

    lax.fori_loop(0, TILES, spread, 0)
    arrived(ag_recv.at[0], line_a.at[0 : N - 1])
    arrived(ag_recv.at[1], line_b.at[0 : N - 1])
    rows_a[y] = line_a[...].reshape(16, SPLIT)
    rows_b[z] = line_b[...].reshape(16, HP - SPLIT)
    for d in FAR:
        remote(rows_a.at[y], rows_a.at[y], ag_send.at[2], ag_recv.at[2], on_y(d))
        remote(rows_b.at[z], rows_b.at[z], ag_send.at[3], ag_recv.at[3], on_z(d))

    prepare(0)
    generate(0)
    arrived(sem_board.at[1], board.at[1])
    prepare(1)
    generate(1)

    arrived(ag_recv.at[2], rows_a.at[0 : N - 1])
    arrived(ag_recv.at[3], rows_b.at[0 : N - 1])

    out_row = lax.broadcasted_iota(jnp.int32, (128, 128), 0)
    in_row = lax.broadcasted_iota(jnp.int32, (128, 128), 1)
    swapped = 16 * ((out_row // 2) % 8) + 2 * (out_row // 16) + out_row % 2
    swap = jnp.where(in_row == swapped, 1.0, 0.0).astype(BF16)
    raw[:, 0:SPLIT] = rows_a[...].reshape(128, SPLIT)
    raw[:, SPLIT:HP] = jnp.dot(swap, rows_b[...].reshape(128, HP - SPLIT), preferred_element_type=F32).astype(BF16)
    tail_lane = lax.broadcasted_iota(jnp.int32, (128, LANES), 1)
    tail = jnp.where(tail_lane == FLAG_LANE, raw[:, TAIL:HP].astype(F32), 0.0)
    shows[...] = jnp.broadcast_to(jnp.sum(tail, axis=1, keepdims=True), (128, 256))

    def build(i, carry):
        rows = pl.ds(pl.multiple_of(i * 16, 16), 16)
        for b in range(4):
            kept = keep[b, rows, :]
            for j in range(TILES):
                cols = slice(j * LANES, (j + 1) * LANES)
                lhs[b, rows, cols] = raw[rows, cols] * kept * row_lv[b, :, cols]
        return carry

    lax.fori_loop(0, N, build, 0)

    part_lane = lax.broadcasted_iota(jnp.int32, (128, 256), 1)

    for b in range(4):
        whole = jnp.dot(lhs[b], cards_left[...], preferred_element_type=F32)
        top = whole.astype(BF16).astype(F32)
        rest = whole - top
        middle = rest.astype(BF16).astype(F32)
        split = jnp.where(part_lane < PARTS[1], top, jnp.where(part_lane < PARTS[2], middle, rest - middle))
        sums[b * 128 : (b + 1) * 128, :] = split.astype(BF16)

    for n, (o, first, width) in enumerate(CHUNKS):
        cols = slice(first, first + width)
        m = n // 2
        folded = jnp.dot(sums[...], cards_right[:, cols], preferred_element_type=F32)
        is_show = shows[:, 0:width] > 0.5
        total = jnp.zeros((128, width), F32)
        for b in range(4):
            shown = jnp.dot(lhs[b], show[b, :, cols], preferred_element_type=F32)
            fold = folded[b * 128 : (b + 1) * 128] + lhs[b, :, cols].astype(F32)
            total += jnp.where(is_show, shown, fold) * board[b // 2, 4 + b % 2 : 5 + b % 2, cols]
        if o == 0:
            part_a[m] = total.reshape(N, N, 2, width)
        else:
            part_b[m, :, 0:width] = total
        for d in FAR:
            if o == 0:
                src, dst, device = part_a.at[m, :, z_peer(d)], recv_a.at[m, d], on_z(d)
            else:
                src = part_b.at[m, pl.ds(pl.multiple_of(y_peer(d) * 16, 16), 16), 0:width]
                dst, device = recv_b.at[m, d, :, 0:width], on_y(d)
            remote(src, dst, rs1_send.at[n], rs1_recv.at[n], device)

    def landed(n):
        o, first, width = CHUNKS[n]
        return recv_a.at[n // 2, 1:N] if o == 0 else recv_b.at[n // 2, 1:N, :, 0:width]

    halves = (slice(0, SPLIT), slice(SPLIT, HP))
    for n, (o, first, width) in enumerate(CHUNKS):
        cols = slice(first, first + width)
        m = n // 2
        arrived(rs1_recv.at[n], landed(n))
        if o == 0:
            total = part_a[m, :, z]
            for d in FAR:
                total += recv_a[m, d]
            mid[:, :, cols] = total
        else:
            total = part_b[m, pl.ds(pl.multiple_of(y * 16, 16), 16), 0:width]
            for d in FAR:
                total += recv_b[m, d, :, 0:width]
            for q in range(N):
                mid[q, :, cols] = total[2 * q : 2 * q + 2]
        if n >= len(CHUNKS) - 2:
            whole = halves[o]
            for d in FAR:
                target, device = (y_peer(d), on_y(d)) if o == 0 else (z_peer(d), on_z(d))
                remote(mid.at[target, :, whole], recv2.at[d, :, whole], rs2_send.at[o], rs2_recv.at[o], device)
    arrived(rs2_recv.at[0], recv2.at[1:N, :, halves[0]])
    arrived(rs2_recv.at[1], recv2.at[1:N, :, halves[1]])
    value_a = mid[y, :, 0:SPLIT]
    value_b = mid[z, :, SPLIT:H]
    for d in FAR:
        value_a += recv2[d, :, 0:SPLIT]
        value_b += recv2[d, :, SPLIT:H]
    row_id = lax.broadcasted_iota(jnp.int32, (2, LANES), 0)
    pots = [pot[0, a].astype(F32) for a in range(2)]
    coefs = [jnp.where(kind[0, a] == 1, -pots[a], pots[a]) * (1.0 / (BOARDS * H)) for a in range(2)]
    coef = jnp.where(row_id == 0, coefs[0], coefs[1])[:, 0:1]
    for first, last, value in ((0, SPLIT, value_a), (SPLIT, H, value_b)):
        worth = value * coef
        held_regret = regrets[:, first:last]
        positive = jnp.maximum(held_regret, 0.0)
        strategy = (positive + FLOOR) / (jnp.sum(positive, axis=0, keepdims=True) + 2 * FLOOR)
        decision = jnp.sum(strategy * worth, axis=0, keepdims=True)
        new_regrets[:, first:last] = jnp.maximum(held_regret + worth - decision, 0.0)
        node[f, :, first:last] = decision

    for d in (2, 1, 3):
        remote(node.at[f], node.at[f], fl_sems.at[0], fl_sems.at[1], (lax.rem(f + d, 4), t, z))
    arrived(fl_sems.at[1], node.at[0:3])
    chance[...] = ((node[0] + node[1]) + (node[2] + node[3])) * 0.25

    arrived(sem_board.at[0], board.at[0])
    arrived(ag_send.at[0], line_a.at[0 : N - 1])
    arrived(ag_send.at[1], line_b.at[0 : N - 1])
    arrived(ag_send.at[2], rows_a.at[0 : N - 1])
    arrived(ag_send.at[3], rows_b.at[0 : N - 1])
    for n in range(len(CHUNKS)):
        arrived(rs1_send.at[n], landed(n))
    for o in range(2):
        arrived(rs2_send.at[o], recv2.at[1:N, :, halves[o]])
    arrived(fl_sems.at[0], node.at[0:3])


def on_device(regrets, opp_reach, pot_size, line_kind, board_lines, board_count, hand_ranks, live_hands):
    vmem = pl.BlockSpec(memory_space=pltpu.VMEM)
    hbm = pl.BlockSpec(memory_space=pltpu.HBM)
    dma = pltpu.SemaphoreType.DMA
    left, right = card_tables()
    updated, chance = pl.pallas_call(
        kernel,
        out_shape=(jax.ShapeDtypeStruct((2, H), F32), jax.ShapeDtypeStruct((1, H), F32)),
        in_specs=[hbm] * 10,
        out_specs=(vmem, vmem),
        scratch_shapes=[
            pltpu.VMEM((2, H), F32),
            pltpu.VMEM((2, H), BF16),
            pltpu.SMEM((1, 2), jnp.int32),
            pltpu.SMEM((1, 2), jnp.int32),
            pltpu.VMEM((2, 256), jnp.int32),
            pltpu.SMEM((1, 2), jnp.int32),
            pltpu.VMEM((2, H), jnp.int32),
            pltpu.VMEM((2, H), jnp.int32),
            pltpu.VMEM((HP, 256), BF16),
            pltpu.VMEM((256, HP), BF16),
            pltpu.VMEM((HP, HP), BF16),
            pltpu.VMEM((HP, HP), BF16),
            pltpu.VMEM((4, HP, HP), BF16),
            pltpu.VMEM((N, 2, SPLIT), BF16),
            pltpu.VMEM((N, 2, HP - SPLIT), BF16),
            pltpu.VMEM((N, 16, SPLIT), BF16),
            pltpu.VMEM((N, 16, HP - SPLIT), BF16),
            pltpu.VMEM((2, 8, HP), F32),
            pltpu.VMEM((4, HP, LANES), BF16),
            pltpu.VMEM((4, HP, LANES), BF16),
            pltpu.VMEM((4, 16, HP), BF16),
            pltpu.VMEM((4, 16, HP), BF16),
            pltpu.VMEM((4, 16, HP), BF16),
            pltpu.VMEM((4, 128, LANES), BF16),
            pltpu.VMEM((128, HP), BF16),
            pltpu.VMEM((128, 256), F32),
            pltpu.VMEM((4, 128, HP), BF16),
            pltpu.VMEM((512, 256), BF16),
            pltpu.VMEM((3, N, N, 2, 256), F32),
            pltpu.VMEM((3, 128, 256), F32),
            pltpu.VMEM((3, N, N, 2, 256), F32),
            pltpu.VMEM((3, N, 16, 256), F32),
            pltpu.VMEM((N, 2, HP), F32),
            pltpu.VMEM((N, 2, HP), F32),
            pltpu.VMEM((4, 1, H), F32),
            dma((10,)),
            dma((2,)),
            dma((4,)),
            dma((4,)),
            dma((6,)),
            dma((6,)),
            dma((2,)),
            dma((2,)),
            dma((2,)),
        ],
        compiler_params=pltpu.CompilerParams(
            collective_id=0, has_side_effects=True, vmem_limit_bytes=48 * 1024 * 1024
        ),
    )(
        *(
            pltpu.with_memory_space_constraint(array, pltpu.HBM)
            for array in (
                regrets[0], opp_reach[0], pot_size, line_kind, board_lines[0, 0], board_count[0],
                hand_ranks[0, 0], live_hands[0, 0], jnp.asarray(left), jnp.asarray(right),
            )
        )
    )
    return updated[None], chance


def solution(mesh):
    lines = ("turn", "river")
    placed = (
        P("flop", lines, None),
        P("flop", lines, None),
        P("flop", lines),
        P("flop", lines),
        P("flop", "turn", "river", None),
        P("flop", "turn", "river"),
        P("flop", "turn", "river", None),
        P("flop", "turn", "river", None),
    )
    return jax.shard_map(
        on_device,
        mesh=mesh,
        in_specs=placed,
        out_specs=(P("flop", lines, None), P(lines, None)),
        check_vma=False,
    )
```
